32 devices in a mesh: gx: 4 (over z), gy: 8 (over y, x, core).
Axes of the slice: x: 2, y: 2, z: 4, core: 2. Of those that a mesh axis runs over, the one named last changes fastest.
Arguments:
- die_basis: float32 [64, 256, 512], P('gx', 'gy'), may hold values from -0.078125 to 0.078125
- die_coeff: float32 [5, 64, 256], P(None, 'gx', 'gy'), may hold values from 0.2 to 5
- pkg_basis: float32 [1024, 64, 512], P(('gx', 'gy')), may hold values from -0.09375 to 0.09375
- send_blocks: int32 [32, 4, 4], P(('gx', 'gy')), may hold values from 0 to 31
- columns: int32 [5, 1024, 4], P(None, ('gx', 'gy')), may hold values from 0 to 47
- counts: int32 [5, 1024], P(None, ('gx', 'gy')), may hold values from 1 to 4
- pkg_blocks: float32 [5, 1024, 64, 256], P(None, ('gx', 'gy')), may hold values from -48 to 48
Outputs:
- reduced: float32 [5, 512, 512], replicated
The draws below stay inside these ranges and needn't reach their ends.
Inputs may be any that keep to these rules, and one draw needn't show every extreme that they name: `columns`: indices below 32 name the partition's own blocks, the others its ghost blocks in the order of the statement.
All inputs are finite; a program needn't handle non-finite values.
Results may differ from the reference program's by a relative error of at most 0.0001.
Values sent between devices are 32-bit elements; how exact they have to be, the bound alone decides.
No kernel may reach another device: no remote copies, remote signals or barrier semaphores. Data moves between devices by JAX's collectives and lax.ppermute only.
A program may use at most 256 MiB of HBM per device.

```python
import math
import jax
import jax.numpy as jnp
from jax import lax

K = 512
TERMS = 5
BLK = 64
NB = 4
GCAP = 4
PB = 32
NDEV = 32
NX = 64
NY = 256
NPB = 1024
N_GX = 4
N_GY = 8


def touch_ends(result, key, least, largest):
    place = [jax.random.randint(jax.random.fold_in(key, axis), (), 0, length) for axis, length in enumerate(result.shape)]
    main_axis = result.shape.index(max(result.shape))
    neighbour = place[:main_axis] + [(place[main_axis] + 1) % result.shape[main_axis]] + place[main_axis + 1:]
    return result.at[tuple(place)].set(least).at[tuple(neighbour)].set(largest)


def spiked(values, own_key, source, target, parts, factor):
    def block_of(axis_at):
        return (jnp.arange(values.shape[axis_at]) // (values.shape[axis_at] // parts)).reshape((-1,) + (1,) * (values.ndim - 1 - axis_at))

    one_side = jax.random.permutation(own_key, parts)[block_of(target)]
    second = (block_of(target) + parts // 2) % parts
    return jnp.where((block_of(source) == one_side) | (block_of(source) == second), factor * values, values)


def shard_levels(stream_key, dims, pieces, smallest, high):
    factor_of = 1.0
    for dim, parts in pieces:
        heights = jax.random.uniform(jax.random.fold_in(jax.random.fold_in(stream_key, 6), dim), (parts,), jnp.float32, smallest / len(pieces), high / len(pieces))
        factor_of = factor_of * jnp.repeat(jnp.exp(heights), dims[dim] // parts).reshape((-1,) + (1,) * (len(dims) - 1 - dim))
    return factor_of


def normal_values(key, dims, scale, most, cuts=(), kind=jnp.bfloat16):
    result = scale * jax.random.normal(key, dims, jnp.float32)
    if cuts:
        result = result * shard_levels(key, dims, cuts, -0.22, 0.18)
    return jnp.clip(result, -most, most).astype(kind)


def gaussian_with(stream_key, extent, deviation, limit, cuts, heavy, held_as=jnp.bfloat16):
    array = deviation * jax.random.normal(stream_key, extent, jnp.float32)
    if cuts:
        array = array * shard_levels(stream_key, extent, cuts, -0.22, 0.18)
    return jnp.clip(spiked(array, jax.random.fold_in(stream_key, 3), *heavy), -limit, limit).astype(held_as)


def setup_inputs(seed: int = 0) -> dict:
    keys = jax.random.split(jax.random.key(seed), 8)
    return {
        "die_basis": gaussian_with(keys[0], (NX, NY, K), ((NX * NY + NPB * BLK) ** -0.5), 0.078125, ((0, 4), (1, 8)), (0, 2, 4, 2.0), jnp.float32),
        "die_coeff": jnp.clip(jnp.exp(math.log(5.0) - 3.218876 * jax.random.uniform(keys[1], (TERMS, NX, NY), jnp.float32) ** shard_levels(keys[1], (TERMS, NX, NY), ((1, 4), (2, 8)), -0.2, 0.2)), 0.2, 5.0),
        "pkg_basis": gaussian_with(keys[2], (NPB, BLK, K), ((NX * NY + NPB * BLK) ** -0.5), 0.09375, ((0, 32),), (0, 2, 32, 2.75), jnp.float32),
        "send_blocks": touch_ends(jax.random.randint(keys[3], (NDEV, 4, GCAP), 0, PB), jax.random.fold_in(keys[3], 1), 0, PB - 1).astype(jnp.int32),
        "columns": touch_ends(jax.random.randint(keys[4], (TERMS, NPB, NB), 0, PB + 4 * GCAP), jax.random.fold_in(keys[4], 1), 0, (PB + 4 * GCAP) - 1).astype(jnp.int32),
        "counts": touch_ends(jax.random.randint(keys[5], (TERMS, NPB), 1, NB + 1), jax.random.fold_in(keys[5], 1), 1, NB).astype(jnp.int32),
        "pkg_blocks": normal_values(keys[6], (TERMS, NPB, BLK, NB * BLK), 8.0, 48.0, ((1, 32),), jnp.float32),
    }


highest = lax.Precision.HIGHEST


def weighted_gram(weights, field):
    width = field.shape[-1]
    flat = field.reshape(-1, width)
    scaled = weights.reshape(-1, 1) * flat
    return lax.dot_general(flat, scaled, (((0,), (0,)), ((), ())), precision=highest, preferred_element_type=jnp.float32)


def die_terms(basis, coeff, next_x_row, next_y_col):
    next_x = jnp.concatenate([basis[1:], next_x_row], axis=0)
    next_y = jnp.concatenate([basis[:, 1:], next_y_col], axis=1)
    diff_x = basis - next_x
    diff_y = basis - next_y
    return jnp.stack([
        weighted_gram(coeff[0], basis),
        weighted_gram(coeff[1], diff_x),
        weighted_gram(coeff[2], diff_y),
        weighted_gram(coeff[3], basis),
        weighted_gram(coeff[4], diff_x) + weighted_gram(coeff[4], diff_y),
    ])


def package_terms(owned, table, columns, counts, blocks):
    row_count = owned.shape[0]
    block = owned.shape[1]
    width = owned.shape[2]
    entries = columns.shape[-1]
    results = []
    for term_idx in range(columns.shape[0]):
        picked = table[columns[term_idx]]
        live = (jnp.arange(entries, dtype=jnp.int32)[None, :] < counts[term_idx][:, None]).astype(jnp.float32)
        matrices = blocks[term_idx].reshape(row_count, block, entries, block) * live[:, None, :, None]
        image = jnp.einsum("rinj,rnjk->rik", matrices, picked, precision=highest)
        results.append(lax.dot_general(owned.reshape(-1, width), image.reshape(-1, width), (((0,), (0,)), ((), ())), precision=highest, preferred_element_type=jnp.float32))
    return jnp.stack(results)


def reference(die_basis, die_coeff, pkg_basis, send_blocks, columns, counts, pkg_blocks):
    zero_row = jnp.zeros((1, NY, K), jnp.float32)
    zero_col = jnp.zeros((NX, 1, K), jnp.float32)
    total = die_terms(die_basis, die_coeff, zero_row, zero_col)

    def local_blocks(source_dev):
        return lax.dynamic_slice_in_dim(pkg_basis, (source_dev * PB).astype(jnp.int32), PB, 0)

    def device_term(dev_idx, accum):
        dev_idx = jnp.asarray(dev_idx).astype(jnp.int32)
        row_a = dev_idx // N_GY
        col_b = dev_idx % N_GY
        sources = [((row_a - 1) % N_GX) * N_GY + col_b, ((row_a + 1) % N_GX) * N_GY + col_b,
                   row_a * N_GY + (col_b - 1) % N_GY, row_a * N_GY + (col_b + 1) % N_GY]
        ghosts = []
        for direction, source_dev in enumerate(sources):
            lists = lax.dynamic_index_in_dim(send_blocks, source_dev.astype(jnp.int32), 0, keepdims=False)
            ghosts.append(local_blocks(source_dev)[lists[direction]])
        owned = local_blocks(dev_idx)
        table = jnp.concatenate([owned] + ghosts, axis=0)
        start = (dev_idx * PB).astype(jnp.int32)
        dev_columns = lax.dynamic_slice_in_dim(columns, start, PB, 1)
        dev_counts = lax.dynamic_slice_in_dim(counts, start, PB, 1)
        dev_blocks = lax.dynamic_slice_in_dim(pkg_blocks, start, PB, 1)
        return accum + package_terms(owned, table, dev_columns, dev_counts, dev_blocks)

    return lax.fori_loop(0, NDEV, device_term, total)
```

```python
import jax
import jax.numpy as jnp
from jax import lax
from jax.sharding import PartitionSpec as P

highest = lax.Precision.HIGH


def from_behind(value, axis, steps):
    count = lax.axis_size(axis)
    leading, last = (max(0, -steps), min(count, count - steps))
    return lax.ppermute(value, axis, [(source, source + steps) for source in range(leading, last)])


def passed_along(value, axis, steps):
    count = lax.axis_size(axis)
    pairs = [(source, (source + steps) % count) for source in range(count)]
    return lax.ppermute(value, axis, pairs)


def weighted_gram(weights, field):
    width = field.shape[-1]
    flat = field.reshape(-1, width)
    scaled = weights.reshape(-1, 1) * flat
    return lax.dot_general(
        flat,
        scaled,
        (((0,), (0,)), ((), ())),
        precision=highest,
        preferred_element_type=jnp.float32,
    )


def die_terms(basis, coeff, next_x_row, next_y_col):
    next_x = jnp.concatenate([basis[1:], next_x_row], axis=0)
    next_y = jnp.concatenate([basis[:, 1:], next_y_col], axis=1)
    diff_x = basis - next_x
    diff_y = basis - next_y
    return jnp.stack(
        [
            weighted_gram(coeff[0], basis),
            weighted_gram(coeff[1], diff_x),
            weighted_gram(coeff[2], diff_y),
            weighted_gram(coeff[3], basis),
            weighted_gram(coeff[4], diff_x) + weighted_gram(coeff[4], diff_y),
        ]
    )


def package_terms(owned, table, columns, counts, blocks):
    row_count = owned.shape[0]
    block = owned.shape[1]
    width = owned.shape[2]
    entries = columns.shape[-1]
    results = []
    for term_idx in range(columns.shape[0]):
        picked = table[columns[term_idx]]
        live = (jnp.arange(entries, dtype=jnp.int32)[None, :] < counts[term_idx][:, None]).astype(
            jnp.float32
        )
        matrices = (
            blocks[term_idx].reshape(row_count, block, entries, block) * live[:, None, :, None]
        )
        image = jnp.einsum("rinj,rnjk->rik", matrices, picked, precision=highest)
        results.append(
            lax.dot_general(
                owned.reshape(-1, width),
                image.reshape(-1, width),
                (((0,), (0,)), ((), ())),
                precision=highest,
                preferred_element_type=jnp.float32,
            )
        )
    return jnp.stack(results)


def body(die_basis, die_coeff, pkg_basis, send_blocks, columns, counts, pkg_blocks):
    next_x_row = from_behind(die_basis[:1], "gx", -1)
    next_y_col = from_behind(die_basis[:, :1], "gy", -1)
    lists = send_blocks[0]
    from_lower_x = passed_along(pkg_basis[lists[0]], "gx", 1)
    from_upper_x = passed_along(pkg_basis[lists[1]], "gx", -1)
    from_lower_y = passed_along(pkg_basis[lists[2]], "gy", 1)
    from_upper_y = passed_along(pkg_basis[lists[3]], "gy", -1)
    table = jnp.concatenate(
        [pkg_basis, from_lower_x, from_upper_x, from_lower_y, from_upper_y], axis=0
    )
    partial_terms = die_terms(die_basis, die_coeff, next_x_row, next_y_col)
    partial_terms = partial_terms + package_terms(pkg_basis, table, columns, counts, pkg_blocks)
    return total_of(partial_terms)


def flip(value, axis, mask):
    count = lax.axis_size(axis)
    return lax.ppermute(value, axis, [(i, i ^ mask) for i in range(count)])


def side(axis, mask):
    return (lax.axis_index(axis) // mask) % 2


def halve(value, dim):
    axis, mask = dim
    mine = side(axis, mask)
    halves = value.reshape((2, value.shape[0] // 2) + value.shape[1:])
    send = lax.dynamic_index_in_dim(halves, 1 - mine, 0, keepdims=False)
    keep = lax.dynamic_index_in_dim(halves, mine, 0, keepdims=False)
    return keep + flip(send, axis, mask)


def double(value, dim):
    axis, mask = dim
    other = flip(value, axis, mask)
    low = jnp.concatenate([value, other], axis=0)
    high = jnp.concatenate([other, value], axis=0)
    return jnp.where(side(axis, mask) == 0, low, high)


def masks(axis):
    count = lax.axis_size(axis)
    return [(axis, 1 << k) for k in range(count.bit_length() - 1)]


def total_of(terms):
    flat = terms.reshape(-1, terms.shape[-1])
    core, *plane = masks("gy")
    line = masks("gx")
    orders = [plane + line, plane[1:] + line + plane[:1], line + plane]
    flat = halve(flat, core)
    rows = flat.shape[0]
    unit = 8 << len(plane + line)
    if rows % unit or rows // unit < 3:
        orders, sizes = orders[:1], [rows]
    else:
        each = rows // unit // 3
        sizes = [rows - 2 * each * unit, each * unit, each * unit]
    starts = [sum(sizes[:k]) for k in range(len(sizes))]
    parts = [lax.slice_in_dim(flat, a, a + n) for a, n in zip(starts, sizes)]
    stages = len(plane + line)
    for k in range(stages):
        parts = [halve(p, o[k]) for p, o in zip(parts, orders)]
    for k in reversed(range(stages)):
        parts = [double(p, o[k]) for p, o in zip(parts, orders)]
    return double(jnp.concatenate(parts, axis=0), core).reshape(terms.shape)


def solution(mesh):
    placed = (
        P("gx", "gy", None),
        P(None, "gx", "gy"),
        P(("gx", "gy"), None, None),
        P(("gx", "gy"), None, None),
        P(None, ("gx", "gy"), None),
        P(None, ("gx", "gy")),
        P(None, ("gx", "gy"), None, None),
    )
    return jax.shard_map(body, mesh=mesh, in_specs=placed, out_specs=P(), check_vma=False)
```

```python
import jax
import jax.numpy as jnp
from jax import lax
from jax.experimental import pallas as pl
from jax.experimental.pallas import tpu as pltpu
from jax.sharding import PartitionSpec as P

ROWS = 4
BF16 = jnp.bfloat16
F32 = jnp.float32


def from_behind(value, axis, steps):
    count = lax.axis_size(axis)
    leading, last = (max(0, -steps), min(count, count - steps))
    return lax.ppermute(value, axis, [(source, source + steps) for source in range(leading, last)])


def passed_along(value, axis, steps):
    count = lax.axis_size(axis)
    pairs = [(source, (source + steps) % count) for source in range(count)]
    return lax.ppermute(value, axis, pairs)


def split(value):
    high = value.astype(BF16)
    return high, (value - high.astype(F32)).astype(BF16)


def mm(a, b):
    return lax.dot_general(a, b, (((1,), (0,)), ((), ())), preferred_element_type=F32)


def gather_kernel(lists, table, *rest):
    outs, sem = rest[:-1], rest[-1]
    copies = []
    for side_index, out in enumerate(outs):
        for k in range(out.shape[0]):
            copies.append(
                pltpu.make_async_copy(
                    table.at[lists[side_index, k]], out.at[k], sem.at[side_index, k]
                )
            )
    for copy in copies:
        copy.start()
    for copy in copies:
        copy.wait()


def gather_sends(table, lists):
    sides, cap = lists.shape
    shape = jax.ShapeDtypeStruct((cap,) + table.shape[1:], table.dtype)
    return pl.pallas_call(
        gather_kernel,
        out_shape=[shape] * sides,
        grid_spec=pltpu.PrefetchScalarGridSpec(
            num_scalar_prefetch=1,
            grid=(),
            in_specs=[pl.BlockSpec(memory_space=pl.ANY)],
            out_specs=[pl.BlockSpec(memory_space=pl.ANY)] * sides,
            scratch_shapes=[pltpu.SemaphoreType.DMA((sides, cap))],
        ),
        name="gather_sends",
    )(lists, table)


def own_kernel(owned, high, low, turned):
    group, block, width = owned.shape
    value = owned[...]
    top, rest = split(value)
    high[...] = top
    low[...] = rest
    flat = value.reshape(group * block, width)
    t_high, t_low = split(flat.T)
    turned[0, :, : group * block] = t_high
    turned[0, :, group * block :] = t_low


def split_own(owned, entries):
    count, block, width = owned.shape
    steps = count // ROWS
    depth = ROWS * block
    table = jax.ShapeDtypeStruct((entries, block, width), BF16)
    table_spec = pl.BlockSpec((ROWS, block, width), lambda i: (i, 0, 0))
    return pl.pallas_call(
        own_kernel,
        out_shape=[table, table, jax.ShapeDtypeStruct((steps, width, 2 * depth), BF16)],
        grid=(steps,),
        in_specs=[table_spec],
        out_specs=[
            table_spec,
            table_spec,
            pl.BlockSpec((1, width, 2 * depth), lambda i: (i, 0, 0)),
        ],
        name="split_own",
    )(owned)


def ghost_kernel(*refs):
    ghosts, high, low = refs[:-4], refs[-2], refs[-1]
    for k, ghost in enumerate(ghosts):
        @pl.when(pl.program_id(0) == k)
        def _():
            top, rest = split(ghost[...])
            high[...] = top
            low[...] = rest


def split_ghosts(ghosts, high, low, count):
    cap, block, width = ghosts[0].shape
    whole = pl.BlockSpec(ghosts[0].shape, lambda i: (0, 0, 0))
    out_spec = pl.BlockSpec(ghosts[0].shape, lambda i: (count // cap + i, 0, 0))
    n = len(ghosts)
    return pl.pallas_call(
        ghost_kernel,
        out_shape=[jax.ShapeDtypeStruct(high.shape, BF16)] * 2,
        grid=(n,),
        in_specs=[whole] * n + [pl.BlockSpec(memory_space=pl.ANY)] * 2,
        out_specs=[out_spec] * 2,
        input_output_aliases={n: 0, n + 1: 1},
        name="split_ghosts",
    )(*ghosts, high, low)


def die_kernel(basis, next_row, next_col, fields, turned):
    nx, ny, width = basis.shape
    value = basis[...]
    below = jnp.concatenate([value[1:], next_row[...]], axis=0)
    right = jnp.concatenate([value[:, 1:], next_col[...]], axis=1)
    for k, field in enumerate((value, value - below, value - right)):
        flat = field.reshape(nx * ny, width)
        fields[k] = flat
        t_high, t_low = split(flat.T)
        turned[k, :, : nx * ny] = t_high
        turned[k, :, nx * ny :] = t_low


def split_die(basis, next_row, next_col):
    nx, ny, width = basis.shape
    cells = nx * ny
    return pl.pallas_call(
        die_kernel,
        out_shape=[
            jax.ShapeDtypeStruct((3, cells, width), F32),
            jax.ShapeDtypeStruct((3, width, 2 * cells), BF16),
        ],
        name="split_die",
    )(basis, next_row, next_col)


def gram(turned, weights, field):
    cells = field.shape[0]
    w_high, w_low = split(weights * field)
    t_high, t_low = turned[:, :cells], turned[:, cells:]
    return mm(t_high, w_high) + mm(t_low, w_high) + mm(t_high, w_low)


def term_kernel(
    columns, counts, fields, die_turned, weights, turned, high, low, blocks, out,
    image_high, image_low, *, first, picks,
):
    term = first + pl.program_id(0)
    count = blocks.shape[1]
    block, wide = blocks.shape[2:]
    entries = wide // block
    groups = turned.shape[0]
    per = count // groups
    depth = per * block
    width = out.shape[2]
    lane = lax.broadcasted_iota(jnp.int32, (block, wide), 1)

    def image_rows(group, slot):
        for k in range(per):
            row = group * per + k
            picked = [columns[term, row * entries + e] for e in range(entries)]
            live = counts[term, row] * block
            matrix = jnp.where(lane < live, blocks[0, row], 0.0)
            a_high, a_low = split(matrix)
            b_high = jnp.concatenate([high[c] for c in picked], axis=0)
            b_low = jnp.concatenate([low[c] for c in picked], axis=0)
            both = mm(jnp.concatenate([a_high, a_low], axis=0), b_high)
            image = both[:block] + both[block:] + mm(a_high, b_low)
            top, rest = split(image)
            image_high[slot, k * block : (k + 1) * block, :] = top
            image_low[slot, k * block : (k + 1) * block, :] = rest

    def project(group, slot):
        top, rest = image_high[slot], image_low[slot]
        pair = turned[group]
        left = jnp.concatenate([pair, pair[:, :depth]], axis=1)
        right = jnp.concatenate([top, top, rest], axis=0)
        out[0] += mm(left, right)

    image_rows(0, 0)
    for which, (q, die) in enumerate(picks):
        @pl.when(term == q)
        def _():
            total = gram(die_turned[die[0]], weights[0], fields[die[0]])
            for k in die[1:]:
                total += gram(die_turned[k], weights[0], fields[k])
            out[0] = total

    def step(group, carry):
        project(group - 1, (group - 1) % 2)
        image_rows(group, group % 2)
        return carry

    lax.fori_loop(1, groups, step, 0)
    project(groups - 1, (groups - 1) % 2)


DIE_FIELDS = ((0,), (1,), (2,), (0,), (1, 2))


def project_terms(first, number, columns, counts, fields, die_turned, weights, turned, high, low, blocks):
    terms, count, block, wide = blocks.shape
    width = high.shape[2]
    depth = turned.shape[2] // 2
    picks = tuple((q, DIE_FIELDS[q]) for q in range(first, first + number))

    def whole(array):
        return pl.BlockSpec(array.shape, lambda i, *_: (0,) * array.ndim, pipeline_mode=pl.Buffered(1))

    def kernel(*refs):
        term_kernel(*refs, first=first, picks=picks)

    return pl.pallas_call(
        kernel,
        out_shape=jax.ShapeDtypeStruct((number, width, width), F32),
        grid_spec=pltpu.PrefetchScalarGridSpec(
            num_scalar_prefetch=2,
            grid=(number,),
            in_specs=[
                whole(fields),
                whole(die_turned),
                pl.BlockSpec((1,) + weights.shape[1:], lambda i, *_: (first + i, 0, 0)),
                whole(turned),
                whole(high),
                whole(low),
                pl.BlockSpec((1, count, block, wide), lambda i, *_: (first + i, 0, 0, 0)),
            ],
            out_specs=pl.BlockSpec((1, width, width), lambda i, *_: (i, 0, 0)),
            scratch_shapes=[pltpu.VMEM((2, depth, width), BF16)] * 2,
        ),
        compiler_params=pltpu.CompilerParams(vmem_limit_bytes=60 << 20),
        name=f"terms_{first}_{number}",
    )(columns, counts, fields, die_turned, weights, turned, high, low, blocks)


def flip(value, axis, mask):
    count = lax.axis_size(axis)
    return lax.ppermute(value, axis, [(i, i ^ mask) for i in range(count)])


def side(axis, mask):
    return (lax.axis_index(axis) // mask) % 2


def halve(value, dim):
    axis, mask = dim
    mine = side(axis, mask)
    halves = value.reshape((2, value.shape[0] // 2) + value.shape[1:])
    send = lax.dynamic_index_in_dim(halves, 1 - mine, 0, keepdims=False)
    keep = lax.dynamic_index_in_dim(halves, mine, 0, keepdims=False)
    return keep + flip(send, axis, mask)


def double(value, dim):
    axis, mask = dim
    other = flip(value, axis, mask)
    low = jnp.concatenate([value, other], axis=0)
    high = jnp.concatenate([other, value], axis=0)
    return jnp.where(side(axis, mask) == 0, low, high)


def masks(axis):
    count = lax.axis_size(axis)
    return [(axis, 1 << k) for k in range(count.bit_length() - 1)]


def total_of(terms):
    flat = terms.reshape(-1, terms.shape[-1])
    core, *plane = masks("gy")
    line = masks("gx")
    orders = [plane + line, plane[1:] + line + plane[:1], line + plane]
    flat = halve(flat, core)
    rows = flat.shape[0]
    unit = 8 << len(plane + line)
    if rows % unit or rows // unit < 3:
        orders, sizes = orders[:1], [rows]
    else:
        each = rows // unit // 3
        sizes = [rows - 2 * each * unit, each * unit, each * unit]
    starts = [sum(sizes[:k]) for k in range(len(sizes))]
    parts = [lax.slice_in_dim(flat, a, a + n) for a, n in zip(starts, sizes)]
    stages = len(plane + line)
    for k in range(stages):
        parts = [halve(p, o[k]) for p, o in zip(parts, orders)]
    for k in reversed(range(stages)):
        parts = [double(p, o[k]) for p, o in zip(parts, orders)]
    return double(jnp.concatenate(parts, axis=0), core).reshape(terms.shape)


def body(die_basis, die_coeff, pkg_basis, send_blocks, columns, counts, pkg_blocks):
    next_x_row = from_behind(die_basis[:1], "gx", -1)
    next_y_col = from_behind(die_basis[:, :1], "gy", -1)
    lists = send_blocks[0]
    sends = gather_sends(pkg_basis, lists)
    ghosts = [
        passed_along(sends[0], "gx", 1),
        passed_along(sends[1], "gx", -1),
        passed_along(sends[2], "gy", 1),
        passed_along(sends[3], "gy", -1),
    ]
    count = pkg_basis.shape[0]
    terms = columns.shape[0]
    high, low, turned = split_own(pkg_basis, count + lists.shape[0] * lists.shape[1])
    fields, die_turned = split_die(die_basis, next_x_row, next_y_col)
    high, low = split_ghosts(ghosts, high, low, count)
    weights = die_coeff.reshape(terms, -1, 1)
    columns = columns.reshape(terms, -1)
    parts = project_terms(
        0, terms, columns, counts, fields, die_turned, weights, turned, high, low, pkg_blocks
    )
    return total_of(parts)


def solution(mesh):
    placed = (
        P("gx", "gy", None),
        P(None, "gx", "gy"),
        P(("gx", "gy"), None, None),
        P(("gx", "gy"), None, None),
        P(None, ("gx", "gy"), None),
        P(None, ("gx", "gy")),
        P(None, ("gx", "gy"), None, None),
    )
    return jax.shard_map(body, mesh=mesh, in_specs=placed, out_specs=P(), check_vma=False)
```

```python
import jax
import jax.numpy as jnp
from jax import lax
from jax.experimental import pallas as pl
from jax.experimental.pallas import tpu as pltpu
from jax.sharding import PartitionSpec as P

ROWS = 4
BF16 = jnp.bfloat16
F32 = jnp.float32


def from_behind(value, axis, steps):
    count = lax.axis_size(axis)
    leading, last = (max(0, -steps), min(count, count - steps))
    return lax.ppermute(value, axis, [(source, source + steps) for source in range(leading, last)])


def passed_along(value, axis, steps):
    count = lax.axis_size(axis)
    pairs = [(source, (source + steps) % count) for source in range(count)]
    return lax.ppermute(value, axis, pairs)


def split(value):
    high = value.astype(BF16)
    return high, (value - high.astype(F32)).astype(BF16)


def mm(a, b):
    return lax.dot_general(a, b, (((1,), (0,)), ((), ())), preferred_element_type=F32)


def gather_kernel(lists, table, *rest):
    outs, sem = rest[:-1], rest[-1]
    copies = []
    for side_index, out in enumerate(outs):
        for k in range(out.shape[0]):
            copies.append(
                pltpu.make_async_copy(
                    table.at[lists[side_index, k]], out.at[k], sem.at[side_index, k]
                )
            )
    for copy in copies:
        copy.start()
    for copy in copies:
        copy.wait()


def gather_sends(table, lists):
    sides, cap = lists.shape
    shape = jax.ShapeDtypeStruct((cap,) + table.shape[1:], table.dtype)
    return pl.pallas_call(
        gather_kernel,
        out_shape=[shape] * sides,
        grid_spec=pltpu.PrefetchScalarGridSpec(
            num_scalar_prefetch=1,
            grid=(),
            in_specs=[pl.BlockSpec(memory_space=pl.ANY)],
            out_specs=[pl.BlockSpec(memory_space=pltpu.VMEM)] * sides,
            scratch_shapes=[pltpu.SemaphoreType.DMA((sides, cap))],
        ),
        name="gather_sends",
    )(lists, table)


def own_kernel(owned, high, low, turned):
    group, block, width = owned.shape
    value = owned[...]
    top, rest = split(value)
    high[...] = top
    low[...] = rest
    flat = value.reshape(group * block, width)
    t_high, t_low = split(flat.T)
    turned[0, :, : group * block] = t_high
    turned[0, :, group * block :] = t_low


def split_own(owned, entries):
    count, block, width = owned.shape
    steps = count // ROWS
    depth = ROWS * block
    table = jax.ShapeDtypeStruct((entries, block, width), BF16)
    table_spec = pl.BlockSpec((ROWS, block, width), lambda i: (i, 0, 0))
    return pl.pallas_call(
        own_kernel,
        out_shape=[table, table, jax.ShapeDtypeStruct((steps, width, 2 * depth), BF16)],
        grid=(steps,),
        in_specs=[table_spec],
        out_specs=[
            table_spec,
            table_spec,
            pl.BlockSpec((1, width, 2 * depth), lambda i: (i, 0, 0)),
        ],
        name="split_own",
    )(owned)


def ghost_kernel(*refs):
    ghosts, high, low = refs[:-4], refs[-2], refs[-1]
    for k, ghost in enumerate(ghosts):
        @pl.when(pl.program_id(0) == k)
        def _():
            top, rest = split(ghost[...])
            high[...] = top
            low[...] = rest


def split_ghosts(ghosts, high, low, count):
    cap, block, width = ghosts[0].shape
    whole = pl.BlockSpec(ghosts[0].shape, lambda i: (0, 0, 0))
    out_spec = pl.BlockSpec(ghosts[0].shape, lambda i: (count // cap + i, 0, 0))
    n = len(ghosts)
    return pl.pallas_call(
        ghost_kernel,
        out_shape=[jax.ShapeDtypeStruct(high.shape, BF16)] * 2,
        grid=(n,),
        in_specs=[whole] * n + [pl.BlockSpec(memory_space=pl.ANY)] * 2,
        out_specs=[out_spec] * 2,
        input_output_aliases={n: 0, n + 1: 1},
        name="split_ghosts",
    )(*ghosts, high, low)


DIE_FIELDS = ((0,), (1,), (2,), (0,), (1, 2))


def die_kernel(basis, next_row, next_col, weights, out, fields, turned):
    nx, ny, width = basis.shape
    cells = nx * ny
    term = pl.program_id(0)

    @pl.when(term == 0)
    def _():
        value = basis[...]
        below = jnp.concatenate([value[1:], next_row[...]], axis=0)
        right = jnp.concatenate([value[:, 1:], next_col[...]], axis=1)
        for k, field in enumerate((value, value - below, value - right)):
            flat = field.reshape(cells, width)
            fields[k] = flat
            t_high, t_low = split(flat.T)
            turned[k, :, :cells] = t_high
            turned[k, :, cells:] = t_low

    def gram(k):
        w_high, w_low = split(weights[0] * fields[k])
        pair = turned[k]
        left = jnp.concatenate([pair, pair[:, :cells]], axis=1)
        return mm(left, jnp.concatenate([w_high, w_high, w_low], axis=0))

    for q, picks in enumerate(DIE_FIELDS):
        @pl.when(term == q)
        def _():
            total = gram(picks[0])
            for k in picks[1:]:
                total += gram(k)
            out[0] = total


def die_parts(basis, next_row, next_col, weights):
    nx, ny, width = basis.shape
    cells = nx * ny
    terms = weights.shape[0]

    def whole(array):
        return pl.BlockSpec(array.shape, lambda i: (0,) * array.ndim)

    return pl.pallas_call(
        die_kernel,
        out_shape=jax.ShapeDtypeStruct((terms, width, width), F32),
        grid=(terms,),
        in_specs=[
            whole(basis),
            whole(next_row),
            whole(next_col),
            pl.BlockSpec((1, cells, 1), lambda i: (i, 0, 0)),
        ],
        out_specs=pl.BlockSpec((1, width, width), lambda i: (i, 0, 0)),
        scratch_shapes=[
            pltpu.VMEM((3, cells, width), F32),
            pltpu.VMEM((3, width, 2 * cells), BF16),
        ],
        cost_estimate=pl.CostEstimate(
            flops=36 * cells * width * width, transcendentals=0, bytes_accessed=8 * terms * width * width
        ),
        name="die_parts",
    )(basis, next_row, next_col, weights)


def term_kernel(
    columns, counts, core, die, turned, high, low, blocks, keep, send,
    total, image_high, image_low, *, first,
):
    term = first + pl.program_id(0)
    mine = core[0]
    count = blocks.shape[1]
    block, wide = blocks.shape[2:]
    entries = wide // block
    groups = turned.shape[0]
    per = count // groups
    depth = per * block
    half = keep.shape[1]
    lane = lax.broadcasted_iota(jnp.int32, (block, wide), 1)

    def image_rows(group, slot):
        for k in range(per):
            row = group * per + k
            picked = [columns[term, row * entries + e] for e in range(entries)]
            live = counts[term, row] * block
            matrix = jnp.where(lane < live, blocks[0, row], 0.0)
            a_high, a_low = split(matrix)
            b_high = jnp.concatenate([high[c] for c in picked], axis=0)
            b_low = jnp.concatenate([low[c] for c in picked], axis=0)
            both = mm(jnp.concatenate([a_high, a_low], axis=0), b_high)
            image = both[:block] + both[block:] + mm(a_high, b_low)
            top, rest = split(image)
            image_high[slot, k * block : (k + 1) * block, :] = top
            image_low[slot, k * block : (k + 1) * block, :] = rest

    def project(group, slot):
        top, rest = image_high[slot], image_low[slot]
        pair = turned[group]
        left = jnp.concatenate([pair, pair[:, :depth]], axis=1)
        right = jnp.concatenate([top, top, rest], axis=0)
        return mm(left, right).reshape(total.shape)

    image_rows(0, 0)
    total[...] = die[0].reshape(total.shape)

    def step(group, carry):
        total[...] += project(group - 1, (group - 1) % 2)
        image_rows(group, group % 2)
        return carry

    lax.fori_loop(1, groups, step, 0)
    total[...] += project(groups - 1, (groups - 1) % 2)
    keep[0] = total[mine]
    send[0] = total[1 - mine]


def project_terms(first, number, columns, counts, core, die, turned, high, low, blocks):
    terms, count, block, wide = blocks.shape
    width = high.shape[2]
    depth = turned.shape[2] // 2
    half = width // 2

    def whole(array):
        return pl.BlockSpec(array.shape, lambda i, *_: (0,) * array.ndim, pipeline_mode=pl.Buffered(1))

    def kernel(*refs):
        term_kernel(*refs, first=first)

    out = jax.ShapeDtypeStruct((number, half, width), F32)
    out_spec = pl.BlockSpec((1, half, width), lambda i, *_: (i, 0, 0))
    return pl.pallas_call(
        kernel,
        out_shape=[out, out],
        grid_spec=pltpu.PrefetchScalarGridSpec(
            num_scalar_prefetch=3,
            grid=(number,),
            in_specs=[
                pl.BlockSpec((1, width, width), lambda i, *_: (first + i, 0, 0)),
                whole(turned),
                whole(high),
                whole(low),
                pl.BlockSpec((1, count, block, wide), lambda i, *_: (first + i, 0, 0, 0)),
            ],
            out_specs=[out_spec, out_spec],
            scratch_shapes=[
                pltpu.VMEM((2, half, width), F32),
                pltpu.VMEM((2, depth, width), BF16),
                pltpu.VMEM((2, depth, width), BF16),
            ],
        ),
        compiler_params=pltpu.CompilerParams(vmem_limit_bytes=40 << 20),
        cost_estimate=pl.CostEstimate(
            flops=8 * number * count * block * width * (wide + width),
            transcendentals=0,
            bytes_accessed=4 * number * (count * block * wide + 2 * width * width),
        ),
        name=f"terms_{first}_{number}",
    )(columns, counts, core, die, turned, high, low, blocks)


def place_kernel(core, mine, other, *refs):
    out = refs[-1]
    half = mine.shape[1]

    @pl.when(core[0] == 0)
    def _():
        out[0, :half] = mine[0]
        out[0, half:] = other[0]

    @pl.when(core[0] == 1)
    def _():
        out[0, :half] = other[0]
        out[0, half:] = mine[0]


def place(core, mine, other, first, terms, filled):
    number, half, width = mine.shape
    spec = pl.BlockSpec((1, half, width), lambda i, *_: (i, 0, 0))
    extra = [] if filled is None else [filled]
    return pl.pallas_call(
        place_kernel,
        out_shape=jax.ShapeDtypeStruct((terms, 2 * half, width), F32),
        grid_spec=pltpu.PrefetchScalarGridSpec(
            num_scalar_prefetch=1,
            grid=(number,),
            in_specs=[spec, spec] + [pl.BlockSpec(memory_space=pl.ANY)] * len(extra),
            out_specs=pl.BlockSpec((1, 2 * half, width), lambda i, *_: (first + i, 0, 0)),
        ),
        input_output_aliases={3: 0} if extra else {},
        name=f"place_{first}",
    )(core, mine, other, *extra)


def flip(value, axis, mask):
    count = lax.axis_size(axis)
    return lax.ppermute(value, axis, [(i, i ^ mask) for i in range(count)])


def side(axis, mask):
    return (lax.axis_index(axis) // mask) % 2


def halve(pair, dim):
    axis, mask = dim
    mine = side(axis, mask)

    def half_of(which):
        picked = [
            lax.dynamic_index_in_dim(
                part.reshape((2, part.shape[0] // 2) + part.shape[1:]), which, 0, keepdims=False
            )
            for part in pair
        ]
        return picked[0] + picked[1]

    return half_of(mine), flip(half_of(1 - mine), axis, mask)


def double(value, dim):
    axis, mask = dim
    other = flip(value, axis, mask)
    low = jnp.concatenate([value, other], axis=0)
    high = jnp.concatenate([other, value], axis=0)
    return jnp.where(side(axis, mask) == 0, low, high)


def masks(axis):
    count = lax.axis_size(axis)
    return [(axis, 1 << k) for k in range(count.bit_length() - 1)]


def chunk_sizes(terms):
    base, extra = divmod(terms, 3)
    return [n for n in (base + (k < extra) for k in range(3)) if n]


def summed(keep, received, order):
    shape = keep.shape
    pair = (keep.reshape(-1, shape[-1]), received.reshape(-1, shape[-1]))
    for dim in order:
        pair = halve(pair, dim)
    value = pair[0] + pair[1]
    for dim in reversed(order):
        value = double(value, dim)
    return value.reshape(shape)


def body(die_basis, die_coeff, pkg_basis, send_blocks, columns, counts, pkg_blocks):
    next_x_row = from_behind(die_basis[:1], "gx", -1)
    next_y_col = from_behind(die_basis[:, :1], "gy", -1)
    lists = send_blocks[0]
    sends = gather_sends(pkg_basis, lists)
    ghosts = [
        passed_along(sends[0], "gx", 1),
        passed_along(sends[1], "gx", -1),
        passed_along(sends[2], "gy", 1),
        passed_along(sends[3], "gy", -1),
    ]
    count = pkg_basis.shape[0]
    terms = columns.shape[0]
    high, low, turned = split_own(pkg_basis, count + lists.shape[0] * lists.shape[1])
    weights = die_coeff.reshape(terms, -1, 1)
    die = die_parts(die_basis, next_x_row, next_y_col, weights)
    high, low = split_ghosts(ghosts, high, low, count)
    columns = columns.reshape(terms, -1)
    (axis, mask), *plane = masks("gy")
    line = masks("gx")
    core = side(axis, mask).astype(jnp.int32).reshape(1)
    orders = [plane + line, plane[1:] + line + plane[:1], line + plane]
    reduced = None
    first = 0
    for number, order in zip(chunk_sizes(terms), orders):
        keep, send = project_terms(
            first, number, columns, counts, core, die, turned, high, low, pkg_blocks
        )
        mine = summed(keep, flip(send, axis, mask), order)
        other = flip(mine, axis, mask)
        reduced = place(core, mine, other, first, terms, reduced)
        first += number
    return reduced


def solution(mesh):
    placed = (
        P("gx", "gy", None),
        P(None, "gx", "gy"),
        P(("gx", "gy"), None, None),
        P(("gx", "gy"), None, None),
        P(None, ("gx", "gy"), None),
        P(None, ("gx", "gy")),
        P(None, ("gx", "gy"), None, None),
    )
    return jax.shard_map(body, mesh=mesh, in_specs=placed, out_specs=P(), check_vma=False)
```

```python
import jax
import jax.numpy as jnp
from jax import lax
from jax.experimental import pallas as pl
from jax.experimental.pallas import tpu as pltpu
from jax.sharding import PartitionSpec as P


ROWS = 4
BF16 = jnp.bfloat16
F32 = jnp.float32


def from_behind(value, axis, steps):
    count = lax.axis_size(axis)
    leading, last = (max(0, -steps), min(count, count - steps))
    return lax.ppermute(value, axis, [(source, source + steps) for source in range(leading, last)])


def passed_along(value, axis, steps):
    count = lax.axis_size(axis)
    pairs = [(source, (source + steps) % count) for source in range(count)]
    return lax.ppermute(value, axis, pairs)


def split(value):
    high = value.astype(BF16)
    return high, (value - high.astype(F32)).astype(BF16)


def mm(a, b):
    return lax.dot_general(a, b, (((1,), (0,)), ((), ())), preferred_element_type=F32)


def gather_kernel(lists, table, first_row, first_col, *refs):
    sides, cap = lists.shape
    outs, (row, col, sems) = refs[:sides], refs[sides:]
    copies = [
        pltpu.make_async_copy(table.at[lists[i, k]], outs[i].at[k], sems.at[i, k])
        for i in range(sides)
        for k in range(cap)
    ]
    for copy in copies:
        copy.start()
    row[...] = first_row[...]
    col[...] = first_col[:, :1]
    for copy in copies:
        copy.wait()


def gather_sends(table, basis, lists):
    sides, cap = lists.shape
    nx, ny, width = basis.shape
    shape = jax.ShapeDtypeStruct((cap,) + table.shape[1:], table.dtype)
    some = min(8, ny)
    return pl.pallas_call(
        gather_kernel,
        out_shape=[shape] * sides
        + [
            jax.ShapeDtypeStruct((1, ny, width), F32),
            jax.ShapeDtypeStruct((nx, 1, width), F32),
        ],
        grid_spec=pltpu.PrefetchScalarGridSpec(
            num_scalar_prefetch=1,
            grid=(1,),
            in_specs=[
                pl.BlockSpec(memory_space=pltpu.HBM),
                pl.BlockSpec((1, ny, width), lambda *_: (0, 0, 0)),
                pl.BlockSpec((nx, some, width), lambda *_: (0, 0, 0)),
            ],
            out_specs=[pl.BlockSpec(shape.shape, lambda *_: (0, 0, 0))] * sides
            + [
                pl.BlockSpec((1, ny, width), lambda *_: (0, 0, 0)),
                pl.BlockSpec((nx, 1, width), lambda *_: (0, 0, 0)),
            ],
            scratch_shapes=[pltpu.SemaphoreType.DMA((sides, cap))],
        ),
        name="gather_sends",
    )(lists, table, basis, basis)


def in_vmem(value):
    return pltpu.with_memory_space_constraint(value, pltpu.VMEM)


def in_hbm(value):
    return pltpu.with_memory_space_constraint(value, pltpu.HBM)


VMEM_SPEC = pl.BlockSpec(memory_space=pltpu.VMEM)


def own_kernel(owned, high, low, turned):
    group, block, width = owned.shape
    at = pl.program_id(0)
    rows = pl.ds(at * group, group)
    value = owned[...]
    top, rest = split(value)
    high[rows] = top
    low[rows] = rest
    flat = value.reshape(group * block, width)
    t_high, t_low = split(flat.T)
    turned[at, :, : group * block] = t_high
    turned[at, :, group * block :] = t_low


def split_own(owned, entries):
    count, block, width = owned.shape
    steps = count // ROWS
    depth = ROWS * block
    table = pltpu.VMEM((entries, block, width), BF16)
    return pl.pallas_call(
        own_kernel,
        out_shape=[table, table, pltpu.VMEM((steps, width, 2 * depth), BF16)],
        grid=(steps,),
        in_specs=[pl.BlockSpec((ROWS, block, width), lambda i: (i, 0, 0))],
        out_specs=[VMEM_SPEC] * 3,
        compiler_params=pltpu.CompilerParams(vmem_limit_bytes=24 << 20),
        name="split_own",
    )(owned)


def ghost_kernel(*refs):
    ghosts, high, low = refs[:-4], refs[-2], refs[-1]
    cap = ghosts[0].shape[0]
    count = high.shape[0] - len(ghosts) * cap
    for k, ghost in enumerate(ghosts):
        top, rest = split(ghost[...])
        high[count + k * cap : count + (k + 1) * cap] = top
        low[count + k * cap : count + (k + 1) * cap] = rest


def add_ghosts(high, low, ghosts):
    n = len(ghosts)
    return pl.pallas_call(
        ghost_kernel,
        out_shape=[pltpu.VMEM(high.shape, BF16)] * 2,
        in_specs=[VMEM_SPEC] * (n + 2),
        out_specs=[VMEM_SPEC] * 2,
        input_output_aliases={n: 0, n + 1: 1},
        compiler_params=pltpu.CompilerParams(vmem_limit_bytes=24 << 20),
        name="add_ghosts",
    )(*[in_vmem(ghost) for ghost in ghosts], in_vmem(high), in_vmem(low))


DIE_FIELDS = ((0,), (1,), (2,), (0,), (1, 2))


def die_kernel(basis, next_row, next_col, weights, out, fields, turned):
    nx, ny, width = basis.shape
    cells = nx * ny
    term = pl.program_id(0)

    @pl.when(term == 0)
    def _():
        value = basis[...]
        below = jnp.concatenate([value[1:], next_row[...]], axis=0)
        right = jnp.concatenate([value[:, 1:], next_col[...]], axis=1)
        for k, field in enumerate((value, value - below, value - right)):
            flat = field.reshape(cells, width)
            fields[k] = flat
            t_high, t_low = split(flat.T)
            turned[k, :, :cells] = t_high
            turned[k, :, cells:] = t_low

    def gram(k):
        w_high, w_low = split((weights[0][:, :, None] * fields[k].reshape(nx, ny, width)).reshape(cells, width))
        pair = turned[k]
        left = jnp.concatenate([pair, pair[:, :cells]], axis=1)
        return mm(left, jnp.concatenate([w_high, w_high, w_low], axis=0))

    for q, picks in enumerate(DIE_FIELDS):
        @pl.when(term == q)
        def _():
            total = gram(picks[0])
            for k in picks[1:]:
                total += gram(k)
            out[0] = total


def die_parts(basis, next_row, next_col, weights):
    nx, ny, width = basis.shape
    cells = nx * ny
    terms = weights.shape[0]

    def whole(array):
        return pl.BlockSpec(array.shape, lambda i: (0,) * array.ndim)

    return pl.pallas_call(
        die_kernel,
        out_shape=jax.ShapeDtypeStruct((terms, width, width), F32),
        grid=(terms,),
        in_specs=[
            whole(basis),
            whole(next_row),
            whole(next_col),
            pl.BlockSpec((1, nx, ny), lambda i: (i, 0, 0)),
        ],
        out_specs=pl.BlockSpec((1, width, width), lambda i: (i, 0, 0)),
        scratch_shapes=[
            pltpu.VMEM((3, cells, width), F32),
            pltpu.VMEM((3, width, 2 * cells), BF16),
        ],
        cost_estimate=pl.CostEstimate(
            flops=36 * cells * width * width, transcendentals=0, bytes_accessed=8 * terms * width * width
        ),
        compiler_params=pltpu.CompilerParams(vmem_limit_bytes=24 << 20),
        name="die_parts",
    )(basis, next_row, next_col, weights)


def term_kernel(
    columns, counts, core, die, blocks, high, low, turned, keep, send,
    total, image_high, image_low, *, first,
):
    term = first + pl.program_id(0)
    mine = core[0]
    count, block, wide = blocks.shape[1:]
    entries = wide // block
    groups = turned.shape[0]
    per = count // groups
    depth = per * block
    lane = lax.broadcasted_iota(jnp.int32, (block, wide), 1)

    def image_rows(group, slot):
        for k in range(per):
            row = group * per + k
            picked = [columns[term, row * entries + e] for e in range(entries)]
            live = counts[term, row] * block
            matrix = jnp.where(lane < live, blocks[0, row], 0.0)
            a_high, a_low = split(matrix)
            b_high = jnp.concatenate([high[c] for c in picked], axis=0)
            b_low = jnp.concatenate([low[c] for c in picked], axis=0)
            both = mm(jnp.concatenate([a_high, a_low], axis=0), b_high)
            image = both[:block] + both[block:] + mm(a_high, b_low)
            top, rest = split(image)
            image_high[slot, k * block : (k + 1) * block, :] = top
            image_low[slot, k * block : (k + 1) * block, :] = rest

    def project(group, slot):
        top, rest = image_high[slot], image_low[slot]
        pair = turned[group]
        left = jnp.concatenate([pair, pair[:, :depth]], axis=1)
        right = jnp.concatenate([top, top, rest], axis=0)
        return mm(left, right).reshape(total.shape)

    image_rows(0, 0)
    total[...] = die[0].reshape(total.shape)

    def step(group, carry):
        total[...] += project(group - 1, (group - 1) % 2)
        image_rows(group, group % 2)
        return carry

    lax.fori_loop(1, groups, step, 0)
    total[...] += project(groups - 1, (groups - 1) % 2)
    keep[0] = total[mine]
    send[0] = total[1 - mine]


def project_terms(first, number, columns, counts, core, die, blocks, high, low, turned):
    _, count, block, wide = blocks.shape
    width = high.shape[2]
    depth = turned.shape[2] // 2
    half = width // 2

    def kernel(*refs):
        term_kernel(*refs, first=first)

    out = jax.ShapeDtypeStruct((number, half, width), F32)
    out_spec = pl.BlockSpec((1, half, width), lambda i, *_: (i, 0, 0))
    return pl.pallas_call(
        kernel,
        out_shape=[out, out],
        grid_spec=pltpu.PrefetchScalarGridSpec(
            num_scalar_prefetch=3,
            grid=(number,),
            in_specs=[
                pl.BlockSpec((1, width, width), lambda i, *_: (first + i, 0, 0)),
                pl.BlockSpec((1, count, block, wide), lambda i, *_: (first + i, 0, 0, 0)),
                VMEM_SPEC,
                VMEM_SPEC,
                VMEM_SPEC,
            ],
            out_specs=[out_spec, out_spec],
            scratch_shapes=[
                pltpu.VMEM((2, half, width), F32),
                pltpu.VMEM((2, depth, width), BF16),
                pltpu.VMEM((2, depth, width), BF16),
            ],
        ),
        compiler_params=pltpu.CompilerParams(vmem_limit_bytes=24 << 20),
        cost_estimate=pl.CostEstimate(
            flops=8 * number * count * block * width * (wide + width),
            transcendentals=0,
            bytes_accessed=4 * number * (count * block * wide + 2 * width * width),
        ),
    )(
        columns, counts, core, in_hbm(die), in_hbm(blocks), in_vmem(high), in_vmem(low),
        in_vmem(turned),
    )


def place_kernel(core, mine, other, *refs):
    out = refs[-1]
    half = mine.shape[1]

    @pl.when(core[0] == 0)
    def _():
        out[0, :half] = mine[0]
        out[0, half:] = other[0]

    @pl.when(core[0] == 1)
    def _():
        out[0, :half] = other[0]
        out[0, half:] = mine[0]


def place(core, mine, other, first, terms, filled):
    number, half, width = mine.shape
    spec = pl.BlockSpec((1, half, width), lambda i, *_: (i, 0, 0))
    extra = [] if filled is None else [filled]
    return pl.pallas_call(
        place_kernel,
        out_shape=jax.ShapeDtypeStruct((terms, 2 * half, width), F32),
        grid_spec=pltpu.PrefetchScalarGridSpec(
            num_scalar_prefetch=1,
            grid=(number,),
            in_specs=[spec, spec] + [pl.BlockSpec(memory_space=pl.ANY)] * len(extra),
            out_specs=pl.BlockSpec((1, 2 * half, width), lambda i, *_: (first + i, 0, 0)),
        ),
        input_output_aliases={3: 0} if extra else {},
    )(core, mine, other, *extra)


def bits(axis):
    count = lax.axis_size(axis)
    return [(axis, 1 << k) for k in range(count.bit_length() - 1)]


def side(dim):
    axis, mask = dim
    return (lax.axis_index(axis) // mask) % 2


def flip(value, dims):
    rows, cols = lax.axis_size("gx"), lax.axis_size("gy")
    pairs = []
    for a in range(rows):
        for b in range(cols):
            axis, mask = dims[b % 2]
            there = (a ^ mask, b) if axis == "gx" else (a, b ^ mask)
            pairs.append((a * cols + b, there[0] * cols + there[1]))
    return lax.ppermute(value, ("gx", "gy"), pairs)


def side_of(dims):
    return jnp.where(lax.axis_index("gy") % 2 == 0, side(dims[0]), side(dims[1]))


def halve(pair, dims):
    mine = side_of(dims)

    def half_of(which):
        picked = [
            lax.dynamic_index_in_dim(
                part.reshape((2, part.shape[0] // 2) + part.shape[1:]), which, 0, keepdims=False
            )
            for part in pair
        ]
        return picked[0] + picked[1]

    return half_of(mine), flip(half_of(1 - mine), dims)


def double(value, dims):
    other = flip(value, dims)
    low = jnp.concatenate([value, other], axis=0)
    high = jnp.concatenate([other, value], axis=0)
    return jnp.where(side_of(dims) == 0, low, high)


CHUNKS = 3


def chunk_sizes(terms):
    base, extra = divmod(terms, CHUNKS)
    return [n for n in (base + (k < extra) for k in range(CHUNKS)) if n]


def summed(keep, received, order):
    shape = keep.shape
    pair = (keep.reshape(-1, shape[-1]), received.reshape(-1, shape[-1]))
    for dim in order:
        pair = halve(pair, dim)
    value = pair[0] + pair[1]
    for dim in reversed(order):
        value = double(value, dim)
    return value.reshape(shape)


def body(die_basis, die_coeff, pkg_basis, send_blocks, columns, counts, pkg_blocks):
    lists = send_blocks[0]
    *sends, row, col = gather_sends(pkg_basis, die_basis, lists)
    next_x_row = from_behind(row, "gx", -1)
    next_y_col = from_behind(col, "gy", -1)
    ghosts = []
    for k, (axis, steps) in enumerate((("gx", 1), ("gx", -1), ("gy", 1), ("gy", -1))):
        ghosts.append(passed_along(sends[k], axis, steps))
    terms = columns.shape[0]
    entries = pkg_basis.shape[0] + lists.shape[0] * lists.shape[1]
    high, low, turned = split_own(pkg_basis, entries)
    die = die_parts(die_basis, next_x_row, next_y_col, die_coeff)
    high, low = add_ghosts(high, low, ghosts)
    columns = columns.reshape(terms, -1)
    pair, *plane = bits("gy")
    line = bits("gx")
    core = side(pair).astype(jnp.int32).reshape(1)
    orders = list(zip(plane + line, plane[1:] + line + plane[:1]))
    reduced = None
    first = 0
    for number in chunk_sizes(terms):
        keep, send = project_terms(
            first, number, columns, counts, core, die, pkg_blocks, high, low, turned
        )
        mine = summed(keep, flip(send, (pair, pair)), orders)
        other = flip(mine, (pair, pair))
        reduced = place(core, mine, other, first, terms, reduced)
        first += number
    return reduced


def solution(mesh):
    placed = (
        P("gx", "gy", None),
        P(None, "gx", "gy"),
        P(("gx", "gy"), None, None),
        P(("gx", "gy"), None, None),
        P(None, ("gx", "gy"), None),
        P(None, ("gx", "gy")),
        P(None, ("gx", "gy"), None, None),
    )
    return jax.shard_map(body, mesh=mesh, in_specs=placed, out_specs=P(), check_vma=False)
```

```python
import jax
import jax.numpy as jnp
from jax import lax
from jax.experimental import pallas as pl
from jax.experimental.pallas import tpu as pltpu
from jax.sharding import PartitionSpec as P


ROWS = 4
BF16 = jnp.bfloat16
F32 = jnp.float32


def from_behind(value, axis, steps):
    count = lax.axis_size(axis)
    leading, last = (max(0, -steps), min(count, count - steps))
    return lax.ppermute(value, axis, [(source, source + steps) for source in range(leading, last)])


def passed_along(value, axis, steps):
    count = lax.axis_size(axis)
    pairs = [(source, (source + steps) % count) for source in range(count)]
    return lax.ppermute(value, axis, pairs)


def split(value):
    high = value.astype(BF16)
    return high, (value - high.astype(F32)).astype(BF16)


def mm(a, b):
    return lax.dot_general(a, b, (((1,), (0,)), ((), ())), preferred_element_type=F32)


def gather_kernel(lists, table, edge, *refs, first):
    outs, (halo, sems) = refs[:-2], refs[-2:]
    copies = [
        pltpu.make_async_copy(table.at[lists[first + i, k]], out.at[k], sems.at[i, k])
        for i, out in enumerate(outs)
        for k in range(out.shape[0])
    ]
    for copy in copies:
        copy.start()
    halo[...] = edge[:, : halo.shape[1]]
    for copy in copies:
        copy.wait()


def gather_sends(table, basis, lists, first, number, along):
    cap = lists.shape[1]
    nx, ny, width = basis.shape
    shape = jax.ShapeDtypeStruct((cap,) + table.shape[1:], table.dtype)
    edge = (1, ny, width) if along == 0 else (nx, min(8, ny), width)
    halo = (1, ny, width) if along == 0 else (nx, 1, width)

    def kernel(*refs):
        gather_kernel(*refs, first=first)

    return pl.pallas_call(
        kernel,
        out_shape=[shape] * number + [jax.ShapeDtypeStruct(halo, F32)],
        grid_spec=pltpu.PrefetchScalarGridSpec(
            num_scalar_prefetch=1,
            grid=(1,),
            in_specs=[
                pl.BlockSpec(memory_space=pltpu.HBM),
                pl.BlockSpec(edge, lambda *_: (0, 0, 0)),
            ],
            out_specs=[pl.BlockSpec(shape.shape, lambda *_: (0, 0, 0))] * number
            + [pl.BlockSpec(halo, lambda *_: (0, 0, 0))],
            scratch_shapes=[pltpu.SemaphoreType.DMA((number, cap))],
        ),
    )(lists, table, basis)


def in_vmem(value):
    return pltpu.with_memory_space_constraint(value, pltpu.VMEM)


def in_hbm(value):
    return pltpu.with_memory_space_constraint(value, pltpu.HBM)


VMEM_SPEC = pl.BlockSpec(memory_space=pltpu.VMEM)


def own_kernel(owned, high, low, turned):
    group, block, width = owned.shape
    at = pl.program_id(0)
    rows = pl.ds(at * group, group)
    value = owned[...]
    top, rest = split(value)
    high[rows] = top
    low[rows] = rest
    flat = value.reshape(group * block, width)
    t_high, t_low = split(flat.T)
    turned[at, :, : group * block] = t_high
    turned[at, :, group * block :] = t_low


def split_own(owned, entries):
    count, block, width = owned.shape
    steps = count // ROWS
    depth = ROWS * block
    table = pltpu.VMEM((entries, block, width), BF16)
    return pl.pallas_call(
        own_kernel,
        out_shape=[table, table, pltpu.VMEM((steps, width, 2 * depth), BF16)],
        grid=(steps,),
        in_specs=[pl.BlockSpec((ROWS, block, width), lambda i: (i, 0, 0))],
        out_specs=[VMEM_SPEC] * 3,
        compiler_params=pltpu.CompilerParams(vmem_limit_bytes=24 << 20),
        name="split_own",
    )(owned)


def ghost_kernel(*refs):
    ghosts, high, low = refs[:-4], refs[-2], refs[-1]
    cap = ghosts[0].shape[0]
    count = high.shape[0] - len(ghosts) * cap
    for k, ghost in enumerate(ghosts):
        top, rest = split(ghost[...])
        high[count + k * cap : count + (k + 1) * cap] = top
        low[count + k * cap : count + (k + 1) * cap] = rest


def add_ghosts(high, low, ghosts):
    n = len(ghosts)
    return pl.pallas_call(
        ghost_kernel,
        out_shape=[pltpu.VMEM(high.shape, BF16)] * 2,
        in_specs=[VMEM_SPEC] * (n + 2),
        out_specs=[VMEM_SPEC] * 2,
        input_output_aliases={n: 0, n + 1: 1},
        compiler_params=pltpu.CompilerParams(vmem_limit_bytes=24 << 20),
        name="add_ghosts",
    )(*[in_vmem(ghost) for ghost in ghosts], in_vmem(high), in_vmem(low))


DIE_FIELDS = ((0,), (1,), (2,), (0,), (1, 2))


def die_kernel(basis, next_row, next_col, weights, out, fields, turned):
    nx, ny, width = basis.shape
    cells = nx * ny
    term = pl.program_id(0)

    @pl.when(term == 0)
    def _():
        value = basis[...]
        below = jnp.concatenate([value[1:], next_row[...]], axis=0)
        right = jnp.concatenate([value[:, 1:], next_col[...]], axis=1)
        for k, field in enumerate((value, value - below, value - right)):
            flat = field.reshape(cells, width)
            fields[k] = flat
            t_high, t_low = split(flat.T)
            turned[k, :, :cells] = t_high
            turned[k, :, cells:] = t_low

    def gram(k):
        w_high, w_low = split((weights[0][:, :, None] * fields[k].reshape(nx, ny, width)).reshape(cells, width))
        pair = turned[k]
        left = jnp.concatenate([pair, pair[:, :cells]], axis=1)
        return mm(left, jnp.concatenate([w_high, w_high, w_low], axis=0))

    for q, picks in enumerate(DIE_FIELDS):
        @pl.when(term == q)
        def _():
            total = gram(picks[0])
            for k in picks[1:]:
                total += gram(k)
            out[0] = total


def die_parts(basis, next_row, next_col, weights):
    nx, ny, width = basis.shape
    cells = nx * ny
    terms = weights.shape[0]

    def whole(array):
        return pl.BlockSpec(array.shape, lambda i: (0,) * array.ndim)

    return pl.pallas_call(
        die_kernel,
        out_shape=jax.ShapeDtypeStruct((terms, width, width), F32),
        grid=(terms,),
        in_specs=[
            whole(basis),
            whole(next_row),
            whole(next_col),
            pl.BlockSpec((1, nx, ny), lambda i: (i, 0, 0)),
        ],
        out_specs=pl.BlockSpec((1, width, width), lambda i: (i, 0, 0)),
        scratch_shapes=[
            pltpu.VMEM((3, cells, width), F32),
            pltpu.VMEM((3, width, 2 * cells), BF16),
        ],
        cost_estimate=pl.CostEstimate(
            flops=36 * cells * width * width, transcendentals=0, bytes_accessed=8 * terms * width * width
        ),
        compiler_params=pltpu.CompilerParams(vmem_limit_bytes=24 << 20),
        name="die_parts",
    )(basis, next_row, next_col, weights)


def term_kernel(
    columns, counts, core, die, blocks, high, low, turned, keep, send,
    total, image_high, image_low, *, first,
):
    term = first + pl.program_id(0)
    mine = core[0]
    count, block, wide = blocks.shape[1:]
    entries = wide // block
    groups = turned.shape[0]
    per = count // groups
    depth = per * block
    lane = lax.broadcasted_iota(jnp.int32, (block, wide), 1)

    def image_rows(group, slot):
        for k in range(per):
            row = group * per + k
            picked = [columns[term, row * entries + e] for e in range(entries)]
            live = counts[term, row] * block
            matrix = jnp.where(lane < live, blocks[0, row], 0.0)
            a_high, a_low = split(matrix)
            b_high = jnp.concatenate([high[c] for c in picked], axis=0)
            b_low = jnp.concatenate([low[c] for c in picked], axis=0)
            both = mm(jnp.concatenate([a_high, a_low], axis=0), b_high)
            image = both[:block] + both[block:] + mm(a_high, b_low)
            top, rest = split(image)
            image_high[slot, k * block : (k + 1) * block, :] = top
            image_low[slot, k * block : (k + 1) * block, :] = rest

    def project(group, slot):
        top, rest = image_high[slot], image_low[slot]
        pair = turned[group]
        left = jnp.concatenate([pair, pair[:, :depth]], axis=1)
        right = jnp.concatenate([top, top, rest], axis=0)
        return mm(left, right).reshape(total.shape)

    image_rows(0, 0)
    total[...] = die[0].reshape(total.shape)

    def step(group, carry):
        total[...] += project(group - 1, (group - 1) % 2)
        image_rows(group, group % 2)
        return carry

    lax.fori_loop(1, groups, step, 0)
    total[...] += project(groups - 1, (groups - 1) % 2)
    keep[0] = total[mine]
    send[0] = total[1 - mine]


def project_terms(first, number, columns, counts, core, die, blocks, high, low, turned):
    _, count, block, wide = blocks.shape
    width = high.shape[2]
    depth = turned.shape[2] // 2
    half = width // 2

    def kernel(*refs):
        term_kernel(*refs, first=first)

    out = jax.ShapeDtypeStruct((number, half, width), F32)
    out_spec = pl.BlockSpec((1, half, width), lambda i, *_: (i, 0, 0))
    return pl.pallas_call(
        kernel,
        out_shape=[out, out],
        grid_spec=pltpu.PrefetchScalarGridSpec(
            num_scalar_prefetch=3,
            grid=(number,),
            in_specs=[
                pl.BlockSpec((1, width, width), lambda i, *_: (first + i, 0, 0)),
                pl.BlockSpec((1, count, block, wide), lambda i, *_: (first + i, 0, 0, 0)),
                VMEM_SPEC,
                VMEM_SPEC,
                VMEM_SPEC,
            ],
            out_specs=[out_spec, out_spec],
            scratch_shapes=[
                pltpu.VMEM((2, half, width), F32),
                pltpu.VMEM((2, depth, width), BF16),
                pltpu.VMEM((2, depth, width), BF16),
            ],
        ),
        compiler_params=pltpu.CompilerParams(vmem_limit_bytes=24 << 20),
        cost_estimate=pl.CostEstimate(
            flops=8 * number * count * block * width * (wide + width),
            transcendentals=0,
            bytes_accessed=4 * number * (count * block * wide + 2 * width * width),
        ),
    )(
        columns, counts, core, in_hbm(die), in_hbm(blocks), in_vmem(high), in_vmem(low),
        in_vmem(turned),
    )


def place_kernel(core, mine, other, *refs):
    out = refs[-1]
    half = mine.shape[1]

    @pl.when(core[0] == 0)
    def _():
        out[0, :half] = mine[0]
        out[0, half:] = other[0]

    @pl.when(core[0] == 1)
    def _():
        out[0, :half] = other[0]
        out[0, half:] = mine[0]


def place(core, mine, other, first, terms, filled):
    number, half, width = mine.shape
    spec = pl.BlockSpec((1, half, width), lambda i, *_: (i, 0, 0))
    extra = [] if filled is None else [filled]
    return pl.pallas_call(
        place_kernel,
        out_shape=jax.ShapeDtypeStruct((terms, 2 * half, width), F32),
        grid_spec=pltpu.PrefetchScalarGridSpec(
            num_scalar_prefetch=1,
            grid=(number,),
            in_specs=[spec, spec] + [pl.BlockSpec(memory_space=pl.ANY)] * len(extra),
            out_specs=pl.BlockSpec((1, 2 * half, width), lambda i, *_: (first + i, 0, 0)),
        ),
        input_output_aliases={3: 0} if extra else {},
    )(core, mine, other, *extra)


def bits(axis):
    count = lax.axis_size(axis)
    return [(axis, 1 << k) for k in range(count.bit_length() - 1)]


def side(dim):
    axis, mask = dim
    return (lax.axis_index(axis) // mask) % 2


def flip(value, dims):
    rows, cols = lax.axis_size("gx"), lax.axis_size("gy")
    pairs = []
    for a in range(rows):
        for b in range(cols):
            axis, mask = dims[b % 2]
            there = (a ^ mask, b) if axis == "gx" else (a, b ^ mask)
            pairs.append((a * cols + b, there[0] * cols + there[1]))
    return lax.ppermute(value, ("gx", "gy"), pairs)


def side_of(dims):
    return jnp.where(lax.axis_index("gy") % 2 == 0, side(dims[0]), side(dims[1]))


def halve(pair, dims):
    mine = side_of(dims)

    def half_of(which):
        picked = [
            lax.dynamic_index_in_dim(
                part.reshape((2, part.shape[0] // 2) + part.shape[1:]), which, 0, keepdims=False
            )
            for part in pair
        ]
        return picked[0] + picked[1]

    return half_of(mine), flip(half_of(1 - mine), dims)


def double(value, dims):
    other = flip(value, dims)
    low = jnp.concatenate([value, other], axis=0)
    high = jnp.concatenate([other, value], axis=0)
    return jnp.where(side_of(dims) == 0, low, high)


SHARES = (2, 2, 1)


def chunk_sizes(terms):
    ends = [terms * sum(SHARES[: k + 1]) // sum(SHARES) for k in range(len(SHARES))]
    return [b - a for a, b in zip([0] + ends, ends)]


def summed(keep, received, order):
    shape = keep.shape
    pair = (keep.reshape(-1, shape[-1]), received.reshape(-1, shape[-1]))
    for dim in order:
        pair = halve(pair, dim)
    value = pair[0] + pair[1]
    for dim in reversed(order):
        value = double(value, dim)
    return value.reshape(shape)


def body(die_basis, die_coeff, pkg_basis, send_blocks, columns, counts, pkg_blocks):
    lists = send_blocks[0]
    *sends, row = gather_sends(pkg_basis, die_basis, lists, 0, 2, 0)
    *more, col = gather_sends(pkg_basis, die_basis, lists, 2, 2, 1)
    sends = sends + more
    next_x_row = from_behind(row, "gx", -1)
    next_y_col = from_behind(col, "gy", -1)
    ghosts = []
    for k, (axis, steps) in enumerate((("gx", 1), ("gx", -1), ("gy", 1), ("gy", -1))):
        ghosts.append(passed_along(sends[k], axis, steps))
    terms = columns.shape[0]
    entries = pkg_basis.shape[0] + lists.shape[0] * lists.shape[1]
    die = die_parts(die_basis, next_x_row, next_y_col, die_coeff)
    owned, die = lax.optimization_barrier((pkg_basis, die))
    high, low, turned = split_own(owned, entries)
    high, low = add_ghosts(high, low, ghosts)
    columns = columns.reshape(terms, -1)
    pair, *plane = bits("gy")
    line = bits("gx")
    core = side(pair).astype(jnp.int32).reshape(1)
    orders = list(zip(plane + line, plane[1:] + line + plane[:1]))
    reduced = None
    first = 0
    for number in chunk_sizes(terms):
        keep, send = project_terms(
            first, number, columns, counts, core, die, pkg_blocks, high, low, turned
        )
        mine = summed(keep, flip(send, (pair, pair)), orders)
        other = flip(mine, (pair, pair))
        reduced = place(core, mine, other, first, terms, reduced)
        first += number
    return reduced


def solution(mesh):
    placed = (
        P("gx", "gy", None),
        P(None, "gx", "gy"),
        P(("gx", "gy"), None, None),
        P(("gx", "gy"), None, None),
        P(None, ("gx", "gy"), None),
        P(None, ("gx", "gy")),
        P(None, ("gx", "gy"), None, None),
    )
    return jax.shard_map(body, mesh=mesh, in_specs=placed, out_specs=P(), check_vma=False)
```

```python
import jax
import jax.numpy as jnp
from jax import lax
from jax.experimental import pallas as pl
from jax.experimental.pallas import tpu as pltpu
from jax.sharding import PartitionSpec as P


ROWS = 4
BF16 = jnp.bfloat16
F32 = jnp.float32


def from_behind(value, axis, steps):
    count = lax.axis_size(axis)
    leading, last = (max(0, -steps), min(count, count - steps))
    return lax.ppermute(value, axis, [(source, source + steps) for source in range(leading, last)])


def passed_along(value, axis, steps):
    count = lax.axis_size(axis)
    pairs = [(source, (source + steps) % count) for source in range(count)]
    return lax.ppermute(value, axis, pairs)


def split(value):
    high = value.astype(BF16)
    return high, (value - high.astype(F32)).astype(BF16)


def mm(a, b):
    return lax.dot_general(a, b, (((1,), (0,)), ((), ())), preferred_element_type=F32)


def gather_kernel(lists, table, edge, *refs, first):
    outs, (halo, sems) = refs[:-2], refs[-2:]
    copies = [
        pltpu.make_async_copy(table.at[lists[first + i, k]], out.at[k], sems.at[i, k])
        for i, out in enumerate(outs)
        for k in range(out.shape[0])
    ]
    for copy in copies:
        copy.start()
    halo[...] = edge[:, : halo.shape[1]]
    for copy in copies:
        copy.wait()


def gather_sends(table, basis, lists, first, number, along):
    cap = lists.shape[1]
    nx, ny, width = basis.shape
    shape = jax.ShapeDtypeStruct((cap,) + table.shape[1:], table.dtype)
    edge = (1, ny, width) if along == 0 else (nx, min(8, ny), width)
    halo = (1, ny, width) if along == 0 else (nx, 1, width)

    def kernel(*refs):
        gather_kernel(*refs, first=first)

    return pl.pallas_call(
        kernel,
        out_shape=[shape] * number + [jax.ShapeDtypeStruct(halo, F32)],
        grid_spec=pltpu.PrefetchScalarGridSpec(
            num_scalar_prefetch=1,
            grid=(1,),
            in_specs=[
                pl.BlockSpec(memory_space=pltpu.HBM),
                pl.BlockSpec(edge, lambda *_: (0, 0, 0)),
            ],
            out_specs=[pl.BlockSpec(shape.shape, lambda *_: (0, 0, 0))] * number
            + [pl.BlockSpec(halo, lambda *_: (0, 0, 0))],
            scratch_shapes=[pltpu.SemaphoreType.DMA((number, cap))],
        ),
    )(lists, table, basis)


def in_vmem(value):
    return pltpu.with_memory_space_constraint(value, pltpu.VMEM)


def in_hbm(value):
    return pltpu.with_memory_space_constraint(value, pltpu.HBM)


VMEM_SPEC = pl.BlockSpec(memory_space=pltpu.VMEM)


def own_kernel(owned, high, low, turned):
    group, block, width = owned.shape
    at = pl.program_id(0)
    rows = pl.ds(at * group, group)
    value = owned[...]
    top, rest = split(value)
    high[rows] = top
    low[rows] = rest
    flat = value.reshape(group * block, width)
    t_high, t_low = split(flat.T)
    turned[at, :, : group * block] = t_high
    turned[at, :, group * block :] = t_low


def split_own(owned, entries):
    count, block, width = owned.shape
    steps = count // ROWS
    depth = ROWS * block
    table = pltpu.VMEM((entries, block, width), BF16)
    return pl.pallas_call(
        own_kernel,
        out_shape=[table, table, pltpu.VMEM((steps, width, 2 * depth), BF16)],
        grid=(steps,),
        in_specs=[pl.BlockSpec((ROWS, block, width), lambda i: (i, 0, 0))],
        out_specs=[VMEM_SPEC] * 3,
        compiler_params=pltpu.CompilerParams(vmem_limit_bytes=24 << 20),
        name="split_own",
    )(owned)


def ghost_kernel(*refs):
    ghosts, high, low = refs[:-4], refs[-2], refs[-1]
    cap = ghosts[0].shape[0]
    count = high.shape[0] - len(ghosts) * cap
    for k, ghost in enumerate(ghosts):
        top, rest = split(ghost[...])
        high[count + k * cap : count + (k + 1) * cap] = top
        low[count + k * cap : count + (k + 1) * cap] = rest


def add_ghosts(high, low, ghosts):
    n = len(ghosts)
    return pl.pallas_call(
        ghost_kernel,
        out_shape=[pltpu.VMEM(high.shape, BF16)] * 2,
        in_specs=[VMEM_SPEC] * (n + 2),
        out_specs=[VMEM_SPEC] * 2,
        input_output_aliases={n: 0, n + 1: 1},
        compiler_params=pltpu.CompilerParams(vmem_limit_bytes=24 << 20),
        name="add_ghosts",
    )(*[in_vmem(ghost) for ghost in ghosts], in_vmem(high), in_vmem(low))


DIE_FIELDS = ((0,), (1,), (2,), (0,), (1, 2))


def die_kernel(basis, next_row, next_col, weights, out, fields, turned):
    nx, ny, width = basis.shape
    cells = nx * ny
    term = pl.program_id(0)

    @pl.when(term == 0)
    def _():
        value = basis[...]
        below = jnp.concatenate([value[1:], next_row[...]], axis=0)
        right = jnp.concatenate([value[:, 1:], next_col[...]], axis=1)
        for k, field in enumerate((value, value - below, value - right)):
            flat = field.reshape(cells, width)
            fields[k] = flat
            t_high, t_low = split(flat.T)
            turned[k, :, :cells] = t_high
            turned[k, :, cells:] = t_low

    def gram(k):
        w_high, w_low = split((weights[0][:, :, None] * fields[k].reshape(nx, ny, width)).reshape(cells, width))
        pair = turned[k]
        left = jnp.concatenate([pair, pair[:, :cells]], axis=1)
        return mm(left, jnp.concatenate([w_high, w_high, w_low], axis=0))

    for q, picks in enumerate(DIE_FIELDS):
        @pl.when(term == q)
        def _():
            total = gram(picks[0])
            for k in picks[1:]:
                total += gram(k)
            out[0] = total


def die_parts(basis, next_row, next_col, weights):
    nx, ny, width = basis.shape
    cells = nx * ny
    terms = weights.shape[0]

    def whole(array):
        return pl.BlockSpec(array.shape, lambda i: (0,) * array.ndim)

    return pl.pallas_call(
        die_kernel,
        out_shape=jax.ShapeDtypeStruct((terms, width, width), F32),
        grid=(terms,),
        in_specs=[
            whole(basis),
            whole(next_row),
            whole(next_col),
            pl.BlockSpec((1, nx, ny), lambda i: (i, 0, 0)),
        ],
        out_specs=pl.BlockSpec((1, width, width), lambda i: (i, 0, 0)),
        scratch_shapes=[
            pltpu.VMEM((3, cells, width), F32),
            pltpu.VMEM((3, width, 2 * cells), BF16),
        ],
        cost_estimate=pl.CostEstimate(
            flops=36 * cells * width * width, transcendentals=0, bytes_accessed=8 * terms * width * width
        ),
        compiler_params=pltpu.CompilerParams(vmem_limit_bytes=24 << 20),
        name="die_parts",
    )(basis, next_row, next_col, weights)


def term_kernel(
    columns, counts, core, die, blocks, high, low, turned, keep, send,
    total, image_high, image_low, *, first,
):
    term = first + pl.program_id(0)
    mine = core[0]
    count, block, wide = blocks.shape[1:]
    entries = wide // block
    groups = turned.shape[0]
    per = count // groups
    depth = per * block
    lane = lax.broadcasted_iota(jnp.int32, (block, wide), 1)

    def image_rows(group, slot):
        for k in range(per):
            row = group * per + k
            picked = [columns[term, row * entries + e] for e in range(entries)]
            live = counts[term, row] * block
            matrix = jnp.where(lane < live, blocks[0, row], 0.0)
            a_high, a_low = split(matrix)
            b_high = jnp.concatenate([high[c] for c in picked], axis=0)
            b_low = jnp.concatenate([low[c] for c in picked], axis=0)
            both = mm(jnp.concatenate([a_high, a_low], axis=0), b_high)
            image = both[:block] + both[block:] + mm(a_high, b_low)
            top, rest = split(image)
            image_high[slot, k * block : (k + 1) * block, :] = top
            image_low[slot, k * block : (k + 1) * block, :] = rest

    def project(group, slot):
        top, rest = image_high[slot], image_low[slot]
        pair = turned[group]
        left = jnp.concatenate([pair, pair[:, :depth]], axis=1)
        right = jnp.concatenate([top, top, rest], axis=0)
        return mm(left, right).reshape(total.shape)

    image_rows(0, 0)
    total[...] = die[0].reshape(total.shape)

    def step(group, carry):
        total[...] += project(group - 1, (group - 1) % 2)
        image_rows(group, group % 2)
        return carry

    lax.fori_loop(1, groups, step, 0)
    total[...] += project(groups - 1, (groups - 1) % 2)
    keep[0] = total[mine]
    send[0] = total[1 - mine]


def project_terms(first, number, columns, counts, core, die, blocks, high, low, turned):
    _, count, block, wide = blocks.shape
    width = high.shape[2]
    depth = turned.shape[2] // 2
    half = width // 2

    def kernel(*refs):
        term_kernel(*refs, first=first)

    out = jax.ShapeDtypeStruct((number, half, width), F32)
    out_spec = pl.BlockSpec((1, half, width), lambda i, *_: (i, 0, 0))
    return pl.pallas_call(
        kernel,
        out_shape=[out, out],
        grid_spec=pltpu.PrefetchScalarGridSpec(
            num_scalar_prefetch=3,
            grid=(number,),
            in_specs=[
                pl.BlockSpec((1, width, width), lambda i, *_: (first + i, 0, 0)),
                pl.BlockSpec((1, count, block, wide), lambda i, *_: (first + i, 0, 0, 0)),
                VMEM_SPEC,
                VMEM_SPEC,
                VMEM_SPEC,
            ],
            out_specs=[out_spec, out_spec],
            scratch_shapes=[
                pltpu.VMEM((2, half, width), F32),
                pltpu.VMEM((2, depth, width), BF16),
                pltpu.VMEM((2, depth, width), BF16),
            ],
        ),
        compiler_params=pltpu.CompilerParams(vmem_limit_bytes=24 << 20),
        cost_estimate=pl.CostEstimate(
            flops=8 * number * count * block * width * (wide + width),
            transcendentals=0,
            bytes_accessed=4 * number * (count * block * wide + 2 * width * width),
        ),
    )(
        columns, counts, core, in_hbm(die), in_hbm(blocks), in_vmem(high), in_vmem(low),
        in_vmem(turned),
    )


def place_kernel(core, mine, other, *refs):
    out = refs[-1]
    half = mine.shape[1]
    at = pl.program_id(0)

    @pl.when(core[0] == 0)
    def _():
        out[0, :half] = mine[at]
        out[0, half:] = other[at]

    @pl.when(core[0] == 1)
    def _():
        out[0, :half] = other[at]
        out[0, half:] = mine[at]


def place(core, mine, other, first, terms, filled):
    number, half, width = mine.shape
    extra = [] if filled is None else [filled]
    return pl.pallas_call(
        place_kernel,
        out_shape=jax.ShapeDtypeStruct((terms, 2 * half, width), F32),
        grid_spec=pltpu.PrefetchScalarGridSpec(
            num_scalar_prefetch=1,
            grid=(number,),
            in_specs=[VMEM_SPEC, VMEM_SPEC] + [pl.BlockSpec(memory_space=pl.ANY)] * len(extra),
            out_specs=pl.BlockSpec((1, 2 * half, width), lambda i, *_: (first + i, 0, 0)),
        ),
        input_output_aliases={3: 0} if extra else {},
        compiler_params=pltpu.CompilerParams(vmem_limit_bytes=16 << 20),
    )(core, in_vmem(mine), in_vmem(other), *extra)


def bits(axis):
    count = lax.axis_size(axis)
    return [(axis, 1 << k) for k in range(count.bit_length() - 1)]


def side(dim):
    axis, mask = dim
    return (lax.axis_index(axis) // mask) % 2


def flip(value, dims):
    rows, cols = lax.axis_size("gx"), lax.axis_size("gy")
    pairs = []
    for a in range(rows):
        for b in range(cols):
            axis, mask = dims[b % 2]
            there = (a ^ mask, b) if axis == "gx" else (a, b ^ mask)
            pairs.append((a * cols + b, there[0] * cols + there[1]))
    return lax.ppermute(value, ("gx", "gy"), pairs)


def side_of(dims):
    return jnp.where(lax.axis_index("gy") % 2 == 0, side(dims[0]), side(dims[1]))


def halve(pair, dims):
    mine = side_of(dims)

    def half_of(which):
        picked = [
            lax.dynamic_index_in_dim(
                part.reshape((2, part.shape[0] // 2) + part.shape[1:]), which, 0, keepdims=False
            )
            for part in pair
        ]
        return picked[0] + picked[1]

    return half_of(mine), flip(half_of(1 - mine), dims)


def double(value, dims):
    other = flip(value, dims)
    low = jnp.concatenate([value, other], axis=0)
    high = jnp.concatenate([other, value], axis=0)
    return jnp.where(side_of(dims) == 0, low, high)


SHARES = (2, 2, 1)


def chunk_sizes(terms):
    ends = [terms * sum(SHARES[: k + 1]) // sum(SHARES) for k in range(len(SHARES))]
    return [b - a for a, b in zip([0] + ends, ends)]


def summed(keep, received, order):
    shape = keep.shape
    pair = (keep.reshape(-1, shape[-1]), received.reshape(-1, shape[-1]))
    for dim in order:
        pair = halve(pair, dim)
    value = pair[0] + pair[1]
    for dim in reversed(order):
        value = double(value, dim)
    return value.reshape(shape)


def body(die_basis, die_coeff, pkg_basis, send_blocks, columns, counts, pkg_blocks):
    lists = send_blocks[0]
    *sends, row = gather_sends(pkg_basis, die_basis, lists, 0, 2, 0)
    *more, col = gather_sends(pkg_basis, die_basis, lists, 2, 2, 1)
    sends = sends + more
    next_x_row = from_behind(row, "gx", -1)
    next_y_col = from_behind(col, "gy", -1)
    ghosts = []
    for k, (axis, steps) in enumerate((("gx", 1), ("gx", -1), ("gy", 1), ("gy", -1))):
        ghosts.append(passed_along(sends[k], axis, steps))
    terms = columns.shape[0]
    entries = pkg_basis.shape[0] + lists.shape[0] * lists.shape[1]
    die = die_parts(die_basis, next_x_row, next_y_col, die_coeff)
    owned, die = lax.optimization_barrier((pkg_basis, die))
    high, low, turned = split_own(owned, entries)
    high, low = add_ghosts(high, low, ghosts)
    columns = columns.reshape(terms, -1)
    pair, *plane = bits("gy")
    line = bits("gx")
    core = side(pair).astype(jnp.int32).reshape(1)
    orders = list(zip(plane + line, plane[1:] + line + plane[:1]))
    reduced = None
    first = 0
    for number in chunk_sizes(terms):
        keep, send = project_terms(
            first, number, columns, counts, core, die, pkg_blocks, high, low, turned
        )
        mine = summed(keep, flip(send, (pair, pair)), orders)
        other = flip(mine, (pair, pair))
        reduced = place(core, mine, other, first, terms, reduced)
        first += number
    return reduced


def solution(mesh):
    placed = (
        P("gx", "gy", None),
        P(None, "gx", "gy"),
        P(("gx", "gy"), None, None),
        P(("gx", "gy"), None, None),
        P(None, ("gx", "gy"), None),
        P(None, ("gx", "gy")),
        P(None, ("gx", "gy"), None, None),
    )
    return jax.shard_map(body, mesh=mesh, in_specs=placed, out_specs=P(), check_vma=False)
```
